1024 devices in a mesh: grid: 64 (over x_hi, z, core), sector: 16 (over x_lo, y).
Axes of the slice: x: 8 (x_hi: 4, x_lo: 2; x = x_hi * 2 + x_lo), y: 8, z: 8, core: 2. Of those that a mesh axis runs over, the one named last changes fastest.
Arguments:
- grid_feat: bfloat16 [131072, 512], P(('grid', 'sector')), may hold values from -6 to 6
- latent: bfloat16 [8192, 1024], P('grid', 'sector'), may hold values from -6 to 6
- query_gain: float32 [512], replicated, may hold values from 0.25 to 1.75
- w_q: bfloat16 [512, 512], replicated, may hold values from -0.25 to 0.25
- w_kv: bfloat16 [1024, 1024], P('sector'), may hold values from -0.1875 to 0.1875
- w_o: bfloat16 [512, 512], replicated, may hold values from -0.25 to 0.25
- head_scale: float32 [8], replicated, may hold values from 0.5 to 80
- block_lists: int32 [1024, 16], P(('grid', 'sector')), may hold values from 0 to 15, as said below
- list_len: int32 [1024], P(('grid', 'sector')), may hold values from 1 to 16, as said below
- dest: int32 [131072], P(('grid', 'sector')), may hold values from 0 to 131071, as said below
Outputs:
- decoded: bfloat16 [131072, 512], P(('grid', 'sector'))
The draws below stay inside these ranges and needn't reach their ends.
Inputs may be any that keep to these rules, and one draw needn't show every extreme that they name: `block_lists`: each row is an ordering of 0 to 16 - 1 (distinct entries); entries at or past list_len are unused. `list_len`: blocks of the first and last band use all 16 entries; other blocks use at least 1 and at most 4 entries. `dest`: A permutation. The point of row r goes to a device (rows over grid+sector) with the same sector index as r's device, and a device's output slot j comes from the device of band j // 2 in its sector; each source sends 2 rows to each device of its sector.
All inputs are finite; a program needn't handle non-finite values.
Results may differ from the reference program's by a relative error of at most 0.013.
The reference program's roundings to bfloat16 on the way (of `lat_kv`, `normed`, `queries`, `probs`, `attended` and `updated`) count: a program that leaves them out, or rounds other values in their place, can miss the bound.
Values may be sent and summed in bfloat16 or wider, within the bound.
No kernel may reach another device: no remote copies, remote signals or barrier semaphores. Data moves between devices by JAX's collectives and lax.ppermute only.
A program may use at most 32 MiB of HBM per device.

```python
import math
import jax
import jax.numpy as jnp
from jax import lax

D_GRID = 512
D_LAT = 1024
HEADS = 8
BLOCK = 128
G_DEV = 128
HEAD_DIM = 64
GROUP = 16
BANDS = 64
SECTORS = 16
NG = 131072
NGB = 1024
NLAT = 8192


def draw_head_scale(key, part):
    return jnp.exp(jax.random.uniform(key, (HEADS,), jnp.float32, math.log(0.5), math.log(2.0)))


def draw_block_lists(key, part):
    raw_scores = jax.random.randint(key, (NGB, GROUP), 0, 1 << 16) * GROUP + jnp.arange(GROUP, dtype=jnp.int32)
    return jnp.argsort(raw_scores, axis=-1).astype(jnp.int32)


def draw_list_len(key, part):
    blocks_per_band = NGB // BANDS
    band_index = jnp.arange(NGB, dtype=jnp.int32) // blocks_per_band
    common = jax.random.randint(key, (NGB,), 1, max(GROUP // 4, 2) + 1)
    polar = (band_index == 0) | (band_index == BANDS - 1)
    return jnp.where(polar, GROUP, common).astype(jnp.int32)


def draw_dest(key, part):
    per_band = G_DEV // BANDS
    raw_scores = jax.random.randint(key, (BANDS * SECTORS, G_DEV), 0, 1 << 16) * G_DEV + jnp.arange(G_DEV, dtype=jnp.int32)
    rank_index = jnp.argsort(jnp.argsort(raw_scores, axis=-1), axis=-1).astype(jnp.int32)
    device = jnp.arange(BANDS * SECTORS, dtype=jnp.int32)[:, None]
    source_band = device // SECTORS
    sector_index = device % SECTORS
    target_band = rank_index // per_band
    slot_index = rank_index % per_band
    target = (target_band * SECTORS + sector_index) * G_DEV + source_band * per_band + slot_index
    return target.reshape(-1).astype(jnp.int32)


def block_scale(rng, shape, split, least, high):
    level = 1.0
    for dim, blocks in split:
        steps = jax.random.uniform(jax.random.fold_in(jax.random.fold_in(rng, 6), dim), (blocks,), jnp.float32, least / len(split), high / len(split))
        level = level * jnp.repeat(jnp.exp(steps), shape[dim] // blocks).reshape((-1,) + (1,) * (len(shape) - 1 - dim))
    return level


def scatter_about(rng, dims, scale, reach, pieces=(), kind=jnp.bfloat16):
    values = scale * jax.random.normal(rng, dims, jnp.float32)
    if pieces:
        values = values * block_scale(rng, dims, pieces, -0.22, 0.18)
    return jnp.clip(values, -reach, reach).astype(kind)


def setup_inputs(seed: int = 0) -> dict:
    key_list = jax.random.split(jax.random.key(seed), 11)
    grid_feat = scatter_about(key_list[0], (NG, D_GRID), 1.0, 6.0, ((0, 1024),))
    latent = scatter_about(key_list[1], (NLAT, D_LAT), 1.0, 6.0, ((0, 64), (1, 16)))
    query_gain = jnp.clip(1.0 + 0.15 * jax.random.normal(key_list[2], (D_GRID,), jnp.float32), 0.25, 1.75)
    w_q = scatter_about(key_list[3], (D_GRID, D_GRID), D_GRID ** -0.5, 0.25)
    w_kv = scatter_about(key_list[4], (D_LAT, 2 * D_GRID), D_LAT ** -0.5, 0.1875, ((0, 16),))
    w_o = scatter_about(key_list[5], (D_GRID, D_GRID), D_GRID ** -0.5, 0.25)
    head_scale = draw_head_scale(jax.random.fold_in(key_list[10], 71), 0)
    block_lists = draw_block_lists(jax.random.fold_in(key_list[10], 71), 0)
    list_len = draw_list_len(jax.random.fold_in(key_list[10], 71), 0)
    dest = draw_dest(jax.random.fold_in(key_list[10], 71), 0)
    return dict(grid_feat=grid_feat, latent=latent, query_gain=query_gain, w_q=w_q, w_kv=w_kv, w_o=w_o, head_scale=head_scale, block_lists=block_lists, list_len=list_len, dest=dest)


def layer_norm(features, gains):
    values = features.astype(jnp.float32)
    centred = values - lax.optimization_barrier(jnp.mean(values, axis=-1, keepdims=True))
    spread = lax.optimization_barrier(jnp.mean(centred * centred, axis=-1, keepdims=True))
    return (centred * lax.rsqrt(spread + 1e-05) * gains).astype(jnp.bfloat16)

def reference(grid_feat, latent, query_gain, w_q, w_kv, w_o, head_scale, block_lists, list_len, dest):
    lat_kv = jnp.dot(latent, w_kv, preferred_element_type=jnp.float32).astype(jnp.bfloat16)
    normed = layer_norm(grid_feat, query_gain)
    queries = jnp.dot(normed, w_q, preferred_element_type=jnp.float32).astype(jnp.bfloat16)
    query_blocks = queries.reshape(NGB, BLOCK, HEADS, HEAD_DIM)
    key_value = lat_kv.reshape(BANDS, BLOCK, 2, HEADS, HEAD_DIM)
    blocks_per_band = NGB // BANDS
    score_scale = head_scale / math.sqrt(HEAD_DIM)

    def one_block(operands):
        block_index, query_block, entries, length = operands
        band_index = block_index // blocks_per_band
        group_start = band_index // GROUP * GROUP
        chosen = key_value[(group_start + entries).astype(jnp.int32)]
        keys = chosen[:, :, 0].reshape(GROUP * BLOCK, HEADS, HEAD_DIM)
        values = chosen[:, :, 1].reshape(GROUP * BLOCK, HEADS, HEAD_DIM)
        scores = jnp.einsum('qhd,khd->hqk', query_block.astype(jnp.float32), keys.astype(jnp.float32))
        scores = scores * score_scale[:, None, None]
        valid = jnp.repeat(jnp.arange(GROUP, dtype=jnp.int32) < length, BLOCK)
        scores = jnp.where(valid[None, None, :], scores, -jnp.inf)
        row_max = lax.optimization_barrier(jnp.max(scores, axis=-1, keepdims=True))
        weights = jnp.exp(scores - row_max)
        denominator = lax.optimization_barrier(jnp.sum(weights, axis=-1))
        probs = weights.astype(jnp.bfloat16)
        weighted = jnp.einsum('hqk,khd->hqd', probs.astype(jnp.float32), values.astype(jnp.float32))
        attended = weighted / denominator[:, :, None]
        return attended.transpose(1, 0, 2).reshape(BLOCK, D_GRID).astype(jnp.bfloat16)
    attended = lax.map(one_block, (jnp.arange(NGB, dtype=jnp.int32), query_blocks, block_lists, list_len))
    attended = attended.reshape(NG, D_GRID)
    updated = (grid_feat.astype(jnp.float32) + jnp.dot(attended, w_o, preferred_element_type=jnp.float32)).astype(jnp.bfloat16)
    return jnp.zeros_like(updated).at[dest].set(updated)
```

```python
import math

import jax
import jax.numpy as jnp
from jax import lax
from jax.experimental import pallas as pl
from jax.experimental.pallas import tpu as pltpu
from jax.sharding import Mesh, PartitionSpec as P

HEADS = 8
BLOCK = 128
HEAD_DIM = 64
HALF = 64
LISTED = 4
ROWS = 136
SECTORS = 16
GROUP = 16

VMEM = pl.BlockSpec(memory_space=pltpu.VMEM)
SMEM = pl.BlockSpec(memory_space=pltpu.SMEM)


def low_lanes(shape):
    return lax.broadcasted_iota(jnp.int32, shape, len(shape) - 1) < HALF


def swap_halves(x):
    return jnp.concatenate([x[:, HALF:], x[:, :HALF]], axis=1)


def pack_kernel(feat_ref, gain_ref, wq_ref, lat_ref, wkv_ref, list_ref, len_ref, out_ref):
    values = feat_ref[...].astype(jnp.float32)
    centred = values - jnp.mean(values, axis=-1, keepdims=True)
    spread = jnp.mean(centred * centred, axis=-1, keepdims=True)
    normed = (centred * lax.rsqrt(spread + 1e-05) * gain_ref[...]).astype(jnp.bfloat16)
    queries = jnp.dot(normed, wq_ref[...], preferred_element_type=jnp.float32).astype(jnp.bfloat16)
    lane = lax.broadcasted_iota(jnp.int32, (8, 128), 1)
    entries = jnp.where(lane == GROUP, len_ref[0], 0)
    for j in range(GROUP):
        entries = jnp.where(lane == j, list_ref[0, j], entries)
    entries = entries.astype(jnp.float32).astype(jnp.bfloat16)
    low = low_lanes((HALF, 128))
    lat = lat_ref[...]
    swapped = swap_halves(lat)
    for head in range(HEADS):
        tile = slice(head // 2 * 128, head // 2 * 128 + 128)
        key_tile = wkv_ref[:, tile]
        value_tile = wkv_ref[:, slice(tile.start + 512, tile.stop + 512)]
        if head % 2:
            piece = jnp.where(low, swap_halves(key_tile), value_tile)
        else:
            piece = jnp.where(low, key_tile, swap_halves(value_tile))
        for half in range(2):
            query = queries[half * HALF:half * HALF + HALF, tile]
            if head % 2:
                query = swap_halves(query)
            peer = half * HEADS + head
            out_ref[peer, 0:HALF] = jnp.where(low, query, lat if half else swapped)
            out_ref[peer, HALF:2 * HALF] = piece
            out_ref[peer, 2 * HALF:ROWS] = entries


def project_kernel(got_ref, out_ref, table_ref):
    latent = got_ref[:, 0:HALF, :].reshape(SECTORS * HALF, 128)
    weights = got_ref[:, HALF:2 * HALF, :].reshape(SECTORS * HALF, 128)
    product = lax.dot_general(latent, weights, (((0,), (0,)), ((), ())), preferred_element_type=jnp.float32)
    panel = product[HALF:].astype(jnp.bfloat16)
    for peer in range(out_ref.shape[0]):
        out_ref[peer] = panel
    for source in range(SECTORS):
        row = got_ref[source, 2 * HALF:ROWS, :].astype(jnp.float32).astype(jnp.int32)
        table_ref[source:source + 1] = row[0:1]


def attend_kernel(table_ref, head_ref, scale_ref, got_ref, panel_ref, out_ref):
    scale = scale_ref[head_ref[0]] * (1.0 / math.sqrt(HEAD_DIM))
    contract_last = (((1,), (1,)), ((), ()))

    def finish(source, weighted, denominator):
        attended = (weighted / denominator).astype(jnp.bfloat16)
        upper, lower = attended[0:32], attended[32:64]
        out_ref[source] = jnp.where(low_lanes((32, 128)), swap_halves(upper), lower)

    def query_of(source):
        tile = got_ref[source, 0:HALF]
        return jnp.where(low_lanes((HALF, 128)), tile, jnp.zeros_like(tile))

    dense = table_ref[0, GROUP] > LISTED

    @pl.when(dense)
    def _():
        per_step = 4

        @pl.loop(0, SECTORS // per_step)
        def _(step):
            keys = panel_ref[...].reshape(GROUP * BLOCK, 128)
            query = jnp.concatenate([query_of(step * per_step + k) for k in range(per_step)], axis=0)
            scores = lax.dot_general(query, keys, contract_last, preferred_element_type=jnp.float32) * scale
            weights = jnp.exp(scores - jnp.max(scores, axis=-1, keepdims=True))
            denominator = jnp.sum(weights, axis=-1, keepdims=True)
            weighted = jnp.dot(weights.astype(jnp.bfloat16), keys, preferred_element_type=jnp.float32)
            for k in range(per_step):
                rows = slice(k * HALF, k * HALF + HALF)
                finish(step * per_step + k, weighted[rows], denominator[rows])

    @pl.when(jnp.logical_not(dense))
    def _():
        def one(source):
            query = query_of(source)
            blocks, scores = [], []
            for j in range(LISTED):
                entry = table_ref[source, j]
                core, column = entry % 2, entry // 2
                block = jnp.concatenate([panel_ref[core, column], panel_ref[core, HEADS + column]], axis=0)
                score = lax.dot_general(query, block, contract_last, preferred_element_type=jnp.float32) * scale
                if j:
                    score = jnp.where(j < table_ref[source, GROUP], score, -jnp.inf)
                blocks.append(block)
                scores.append(score)
            top = scores[0]
            for score in scores[1:]:
                top = jnp.maximum(top, score)
            top = jnp.max(top, axis=-1, keepdims=True)
            weights = [jnp.exp(score - top) for score in scores]
            denominator = jnp.sum(sum(weights[1:], weights[0]), axis=-1, keepdims=True)
            weighted = sum(
                jnp.dot(weight.astype(jnp.bfloat16), block, preferred_element_type=jnp.float32)
                for weight, block in zip(weights, blocks)
            )
            finish(source, weighted, denominator)

        @pl.loop(0, SECTORS // 4)
        def _(step):
            for k in range(4):
                one(step * 4 + k)


def finish_kernel(got_ref, wo_ref, feat_ref, position_ref, out_ref):
    low = low_lanes((32, 128))
    rows = []
    for half in range(2):
        upper, lower = [], []
        for pair in range(HEADS // 2):
            even = got_ref[half * HEADS + 2 * pair]
            odd = got_ref[half * HEADS + 2 * pair + 1]
            upper.append(jnp.where(low, even, swap_halves(odd)))
            lower.append(jnp.where(low, swap_halves(even), odd))
        rows += [jnp.concatenate(upper, axis=1), jnp.concatenate(lower, axis=1)]
    attended = jnp.concatenate(rows, axis=0)
    product = jnp.dot(attended, wo_ref[...], preferred_element_type=jnp.float32)
    updated = (feat_ref[...].astype(jnp.float32) + product).astype(jnp.bfloat16)
    slot = lax.broadcasted_iota(jnp.int32, (BLOCK, BLOCK), 0)
    chosen = (slot == position_ref[...]).astype(jnp.float32).astype(jnp.bfloat16)
    out_ref[...] = jnp.dot(chosen, updated, preferred_element_type=jnp.float32).astype(jnp.bfloat16)


def shards(grid_feat, latent, query_gain, w_q, w_kv, w_o, head_scale, block_lists, list_len, dest):
    band_axes, sector_axes = ("xh", "z", "c"), ("xl", "y")
    band_count = lax.axis_size(band_axes)
    band_index = lax.axis_index(band_axes)
    local_rows, width = grid_feat.shape
    bf16 = jnp.bfloat16

    packed = pl.pallas_call(
        pack_kernel,
        out_shape=jax.ShapeDtypeStruct((SECTORS, ROWS, 128), bf16),
        in_specs=[VMEM, VMEM, VMEM, VMEM, VMEM, SMEM, SMEM],
        out_specs=VMEM,
        name="pack",
    )(grid_feat, query_gain.reshape(1, -1), w_q, latent.T, w_kv, block_lists, list_len)
    got = lax.all_to_all(packed, sector_axes, 0, 0, tiled=True)

    panel, table = pl.pallas_call(
        project_kernel,
        out_shape=(
            jax.ShapeDtypeStruct((GROUP, HALF, 128), bf16),
            jax.ShapeDtypeStruct((SECTORS, 128), jnp.int32),
        ),
        in_specs=[VMEM],
        out_specs=(VMEM, VMEM),
        name="project",
    )(got)
    panels = lax.all_to_all(panel, ("xl", "z"), 0, 0, tiled=True)
    panels = lax.all_gather(panels, "c", axis=0)

    attended = pl.pallas_call(
        attend_kernel,
        out_shape=jax.ShapeDtypeStruct((SECTORS, 32, 128), bf16),
        in_specs=[SMEM, SMEM, SMEM, VMEM, VMEM],
        out_specs=VMEM,
        name="attend",
    )(table, lax.axis_index("y").reshape(1), head_scale, got, panels)
    attended = lax.all_to_all(attended, sector_axes, 0, 0, tiled=True)

    per_band = local_rows // band_count
    position = dest // local_rows // SECTORS * per_band + dest % local_rows - band_index * per_band
    outgoing = pl.pallas_call(
        finish_kernel,
        out_shape=jax.ShapeDtypeStruct((local_rows, width), bf16),
        in_specs=[VMEM, VMEM, VMEM, VMEM],
        out_specs=VMEM,
        name="finish",
    )(attended, w_o, grid_feat, position.reshape(1, -1))
    return lax.all_to_all(outgoing, band_axes, 0, 0, tiled=True)


def solution(mesh):
    fine = Mesh(mesh.devices.reshape(4, 8, 2, 2, 8), ("xh", "z", "c", "xl", "y"))
    band, sector = ("xh", "z", "c"), ("xl", "y")
    return jax.shard_map(
        shards,
        mesh=fine,
        in_specs=(
            P(band + sector, None),
            P(band, sector),
            P(),
            P(),
            P(sector, None),
            P(),
            P(),
            P(band + sector, None),
            P(band + sector),
            P(band + sector),
        ),
        out_specs=P(band + sector, None),
        check_vma=False,
    )
```

```python
import math

import jax
import jax.numpy as jnp
from jax import lax
from jax.experimental import pallas as pl
from jax.experimental.pallas import tpu as pltpu
from jax.sharding import Mesh, PartitionSpec as P

HEADS = 8
BLOCK = 128
HEAD_DIM = 64
HALF = 64
LISTED = 4
PER_DOT = 4
DOTS = 4
UNROLL = 4
LIMIT = 12 << 20
ROWS = 136
SECTORS = 16
GROUP = 16

VMEM = pl.BlockSpec(memory_space=pltpu.VMEM)
SMEM = pl.BlockSpec(memory_space=pltpu.SMEM)
HBM = pl.BlockSpec(memory_space=pltpu.HBM)
PARAMS = pltpu.CompilerParams(vmem_limit_bytes=LIMIT)


def low_lanes(shape):
    return lax.broadcasted_iota(jnp.int32, shape, len(shape) - 1) < HALF


def swap_halves(x):
    return jnp.concatenate([x[:, HALF:], x[:, :HALF]], axis=1)


def pack_kernel(
    feat_hbm, gain_hbm, lat_hbm, wkv_hbm, wq_hbm, list_hbm, len_hbm, dest_hbm, scale_hbm, out_hbm,
    feat_ref, gain_ref, lat_ref, wkv_ref, wq_ref, list_ref, len_ref, dest_ref, scale_ref, row_ref, out_ref, sems, out_sems,
):
    pairs = (
        (feat_hbm, feat_ref), (gain_hbm, gain_ref), (lat_hbm, lat_ref), (wkv_hbm, wkv_ref),
        (wq_hbm, wq_ref), (list_hbm, list_ref), (len_hbm, len_ref), (dest_hbm, dest_ref), (scale_hbm, scale_ref),
    )
    copies = [pltpu.make_async_copy(source, target, sems.at[k]) for k, (source, target) in enumerate(pairs)]
    for copy in copies:
        copy.start()
    for copy in copies[:4]:
        copy.wait()
    values = feat_ref[...].astype(jnp.float32)
    centred = values - jnp.mean(values, axis=-1, keepdims=True)
    spread = jnp.mean(centred * centred, axis=-1, keepdims=True)
    normed = (centred * lax.rsqrt(spread + 1e-05) * gain_ref[...]).astype(jnp.bfloat16)
    for copy in copies[4:]:
        copy.wait()
    queries = jnp.dot(normed, wq_ref[...], preferred_element_type=jnp.float32).astype(jnp.bfloat16)
    lane = lax.broadcasted_iota(jnp.int32, (8, 128), 1)
    row_ref[:, 0:GROUP] = list_ref[...]
    entries = jnp.where(lane < GROUP, jnp.broadcast_to(row_ref[...], (8, 128)), 0)
    entries = jnp.where(lane == GROUP, jnp.broadcast_to(len_ref[...], (8, 128)), entries)
    dest = dest_ref[...]
    position = dest // (BLOCK * SECTORS) * 2 + dest % 2
    row = lax.broadcasted_iota(jnp.int32, (8, 128), 0)
    entries = jnp.where(row == 1, jnp.broadcast_to(position, (8, 128)), entries)
    head_lane = lax.broadcasted_iota(jnp.int32, (1, HEADS), 1)
    own = jnp.where(head_lane == lax.axis_index("y"), scale_ref[...], 0.0)
    own = jnp.broadcast_to(jnp.sum(own, axis=-1, keepdims=True), (8, 128))
    first = own.astype(jnp.bfloat16).astype(jnp.float32)
    second = (own - first).astype(jnp.bfloat16).astype(jnp.float32)
    parts = jnp.where(row == 2, first, jnp.where(row == 3, second, own - first - second))
    entries = jnp.where(row < 2, entries.astype(jnp.float32), parts).astype(jnp.bfloat16)
    low = low_lanes((HALF, 128))
    lat = lat_ref[...]
    swapped = swap_halves(lat)
    sends = []
    for head in range(HEADS):
        tile = slice(head // 2 * 128, head // 2 * 128 + 128)
        key_tile = wkv_ref[:, tile]
        value_tile = wkv_ref[:, slice(tile.start + 512, tile.stop + 512)]
        if head % 2:
            piece = jnp.where(low, swap_halves(key_tile), value_tile)
        else:
            piece = jnp.where(low, key_tile, swap_halves(value_tile))
        for half in range(2):
            query = queries[half * HALF:half * HALF + HALF, tile]
            if head % 2:
                query = swap_halves(query)
            peer = half * HEADS + head
            out_ref[peer, 0:HALF] = jnp.where(low, query, lat if half else swapped)
            out_ref[peer, HALF:2 * HALF] = piece
            out_ref[peer, 2 * HALF:ROWS] = entries
            send = pltpu.make_async_copy(out_ref.at[peer], out_hbm.at[peer], out_sems.at[peer])
            send.start()
            sends.append(send)
    for send in sends:
        send.wait()


def project_kernel(got_ref, out_ref, table_ref, position_ref, scale_ref):
    latent = got_ref[:, 0:HALF, :].reshape(SECTORS * HALF, 128)
    weights = got_ref[:, HALF:2 * HALF, :].reshape(SECTORS * HALF, 128)
    product = lax.dot_general(latent, weights, (((0,), (0,)), ((), ())), preferred_element_type=jnp.float32)
    panel = product[HALF:].astype(jnp.bfloat16)
    for peer in range(out_ref.shape[0]):
        out_ref[peer] = panel
    for source in range(SECTORS):
        row = got_ref[source, 2 * HALF:ROWS, :].astype(jnp.float32).astype(jnp.int32)
        table_ref[source:source + 1] = row[0:1]
    own = got_ref[lax.axis_index(("xl", "y")), 2 * HALF:ROWS, :].astype(jnp.float32)
    position_ref[...] = own[1:2].astype(jnp.int32)
    scale_ref[...] = (own[2:3] + own[3:4]) + own[4:5]


def attend_kernel(table_ref, scale_ref, got_ref, panel_ref, out_ref):
    scale = scale_ref[:, 0:1] * (math.log2(math.e) / math.sqrt(HEAD_DIM))
    contract_last = (((1,), (1,)), ((), ()))

    def finish(source, weighted, denominator):
        attended = (weighted / denominator).astype(jnp.bfloat16)
        upper, lower = attended[0:32], attended[32:64]
        out_ref[source] = jnp.where(low_lanes((32, 128)), swap_halves(upper), lower)

    def query_of(source):
        tile = got_ref[source, 0:HALF]
        return jnp.where(low_lanes((HALF, 128)), tile, jnp.zeros_like(tile))

    dense = table_ref[0, GROUP] > LISTED

    @pl.when(dense)
    def _():
        keys = panel_ref[...].reshape(GROUP * BLOCK, 128)

        def several(first):
            query = jnp.concatenate([query_of(first + k) for k in range(PER_DOT)], axis=0)
            scores = lax.dot_general(query, keys, contract_last, preferred_element_type=jnp.float32)
            weights = jnp.exp2((scores - jnp.max(scores, axis=-1, keepdims=True)) * scale)
            denominator = jnp.sum(weights, axis=-1, keepdims=True)
            weighted = jnp.dot(weights.astype(jnp.bfloat16), keys, preferred_element_type=jnp.float32)
            for k in range(PER_DOT):
                rows = slice(k * HALF, k * HALF + HALF)
                finish(first + k, weighted[rows], denominator[rows])

        @pl.loop(0, SECTORS // (PER_DOT * DOTS))
        def _(step):
            for k in range(DOTS):
                several((step * DOTS + k) * PER_DOT)

    @pl.when(jnp.logical_not(dense))
    def _():
        def one(source):
            query = query_of(source)
            halves = []
            for j in range(LISTED):
                entry = table_ref[source, j]
                core, column = entry % 2, entry // 2
                halves += [panel_ref[core, column], panel_ref[core, HEADS + column]]
            blocks = jnp.concatenate(halves, axis=0)
            scores = lax.dot_general(query, blocks, contract_last, preferred_element_type=jnp.float32)
            column = lax.broadcasted_iota(jnp.int32, scores.shape, 1)
            scores = jnp.where(column < table_ref[source, GROUP] * BLOCK, scores, -jnp.inf)
            weights = jnp.exp2((scores - jnp.max(scores, axis=-1, keepdims=True)) * scale)
            denominator = jnp.sum(weights, axis=-1, keepdims=True)
            weighted = jnp.dot(weights.astype(jnp.bfloat16), blocks, preferred_element_type=jnp.float32)
            finish(source, weighted, denominator)

        @pl.loop(0, SECTORS // UNROLL)
        def _(step):
            for k in range(UNROLL):
                one(step * UNROLL + k)


def finish_kernel(got_ref, wo_ref, feat_ref, position_ref, out_ref):
    low = low_lanes((32, 128))
    rows = []
    for half in range(2):
        upper, lower = [], []
        for pair in range(HEADS // 2):
            even = got_ref[half * HEADS + 2 * pair]
            odd = got_ref[half * HEADS + 2 * pair + 1]
            upper.append(jnp.where(low, even, swap_halves(odd)))
            lower.append(jnp.where(low, swap_halves(even), odd))
        rows += [jnp.concatenate(upper, axis=1), jnp.concatenate(lower, axis=1)]
    attended = jnp.concatenate(rows, axis=0)
    product = jnp.dot(attended, wo_ref[...], preferred_element_type=jnp.float32)
    updated = (feat_ref[...].astype(jnp.float32) + product).astype(jnp.bfloat16)
    slot = lax.broadcasted_iota(jnp.int32, (BLOCK, BLOCK), 0)
    chosen = (slot == position_ref[...]).astype(jnp.float32).astype(jnp.bfloat16)
    moved = jnp.dot(chosen, updated, preferred_element_type=jnp.float32)
    out_ref[...] = moved.reshape(out_ref.shape).astype(jnp.bfloat16)


def shards(grid_feat, latent, query_gain, w_q, w_kv, w_o, head_scale, block_lists, list_len, dest):
    band_axes, sector_axes = ("xh", "z", "c"), ("xl", "y")
    local_rows, width = grid_feat.shape
    bf16 = jnp.bfloat16

    packed = pl.pallas_call(
        pack_kernel,
        out_shape=jax.ShapeDtypeStruct((SECTORS, ROWS, 128), bf16),
        in_specs=[HBM] * 9,
        out_specs=HBM,
        scratch_shapes=[
            pltpu.VMEM((local_rows, width), bf16),
            pltpu.VMEM((1, width), jnp.float32),
            pltpu.VMEM(latent.shape[::-1], bf16),
            pltpu.VMEM(w_kv.shape, bf16),
            pltpu.VMEM(w_q.shape, bf16),
            pltpu.VMEM((1, GROUP), jnp.int32),
            pltpu.VMEM((1, 1), jnp.int32),
            pltpu.VMEM((1, local_rows), jnp.int32),
            pltpu.VMEM((1, HEADS), jnp.float32),
            pltpu.VMEM((1, 128), jnp.int32),
            pltpu.VMEM((SECTORS, ROWS, 128), bf16),
            pltpu.SemaphoreType.DMA((9,)),
            pltpu.SemaphoreType.DMA((SECTORS,)),
        ],
        name="pack",
        compiler_params=pltpu.CompilerParams(vmem_limit_bytes=60 << 20),
    )(
        grid_feat, query_gain.reshape(1, -1), latent.T, w_kv, w_q, block_lists, list_len.reshape(1, 1),
        dest.reshape(1, -1), head_scale.reshape(1, -1),
    )
    got = lax.all_to_all(packed, sector_axes, 0, 0, tiled=True)

    panel, table, position, scale = pl.pallas_call(
        project_kernel,
        out_shape=(
            jax.ShapeDtypeStruct((GROUP, HALF, 128), bf16),
            jax.ShapeDtypeStruct((SECTORS, 128), jnp.int32),
            jax.ShapeDtypeStruct((1, 128), jnp.int32),
            jax.ShapeDtypeStruct((1, 128), jnp.float32),
        ),
        in_specs=[VMEM],
        out_specs=(VMEM,) * 4,
        name="project",
        compiler_params=PARAMS,
    )(got)
    panels = lax.all_to_all(panel, ("xl", "z"), 0, 0, tiled=True)
    panels = lax.all_gather(panels, "c", axis=0)

    attended = pl.pallas_call(
        attend_kernel,
        out_shape=jax.ShapeDtypeStruct((SECTORS, 32, 128), bf16),
        in_specs=[SMEM, VMEM, VMEM, VMEM],
        out_specs=VMEM,
        name="attend",
        compiler_params=PARAMS,
    )(table, scale, got, panels)
    attended = lax.all_to_all(attended, sector_axes, 0, 0, tiled=True)

    outgoing = pl.pallas_call(
        finish_kernel,
        out_shape=jax.ShapeDtypeStruct((local_rows // 2, 2, width), bf16),
        in_specs=[VMEM, VMEM, VMEM, VMEM],
        out_specs=VMEM,
        name="finish",
        compiler_params=PARAMS,
    )(attended, w_o, grid_feat, position)
    arrived = lax.all_to_all(outgoing, band_axes, 0, 0, tiled=True)
    return arrived.reshape(local_rows, width)


def solution(mesh):
    fine = Mesh(mesh.devices.reshape(4, 8, 2, 2, 8), ("xh", "z", "c", "xl", "y"))
    band, sector = ("xh", "z", "c"), ("xl", "y")
    return jax.shard_map(
        shards,
        mesh=fine,
        in_specs=(
            P(band + sector, None),
            P(band, sector),
            P(),
            P(),
            P(sector, None),
            P(),
            P(),
            P(band + sector, None),
            P(band + sector),
            P(band + sector),
        ),
        out_specs=P(band + sector, None),
        check_vma=False,
    )
```

```python
import math

import jax
import jax.numpy as jnp
from jax import lax
from jax.experimental import pallas as pl
from jax.experimental.pallas import tpu as pltpu
from jax.sharding import Mesh, PartitionSpec as P

HEADS = 8
BLOCK = 128
HEAD_DIM = 64
HALF = 64
LISTED = 4
GROUP = 16
SECTORS = 16
SOURCES = 8
ROWS = 200
TAIL = 3 * HALF
PER_DOT = 2

VMEM = pl.BlockSpec(memory_space=pltpu.VMEM)
SMEM = pl.BlockSpec(memory_space=pltpu.SMEM)
HBM = pl.BlockSpec(memory_space=pltpu.HBM)
PARAMS = pltpu.CompilerParams(vmem_limit_bytes=12 << 20)
CONTRACT_LAST = (((1,), (1,)), ((), ()))
CONTRACT_FIRST = (((0,), (0,)), ((), ()))


def low_lanes(rows):
    return lax.broadcasted_iota(jnp.int32, (rows, 128), 1) < HALF


def swap_halves(x):
    return jnp.concatenate([x[:, HALF:], x[:, :HALF]], axis=1)


def pack_kernel(
    feat_hbm, gain_hbm, lat_hbm, wkv_hbm, wq_hbm, list_hbm, len_hbm, dest_hbm, scale_hbm, out_hbm,
    feat_ref, gain_ref, lat_ref, wkv_ref, wq_ref, list_ref, len_ref, dest_ref, scale_ref, row_ref, out_ref,
    sems, out_sems,
):
    pairs = (
        (feat_hbm, feat_ref), (gain_hbm, gain_ref), (lat_hbm, lat_ref), (wkv_hbm, wkv_ref),
        (wq_hbm, wq_ref), (list_hbm, list_ref), (len_hbm, len_ref), (dest_hbm, dest_ref), (scale_hbm, scale_ref),
    )
    copies = [pltpu.make_async_copy(source, target, sems.at[k]) for k, (source, target) in enumerate(pairs)]
    for copy in copies:
        copy.start()
    for copy in copies[:4]:
        copy.wait()
    values = feat_ref[...].astype(jnp.float32)
    centred = values - jnp.mean(values, axis=-1, keepdims=True)
    spread = jnp.mean(centred * centred, axis=-1, keepdims=True)
    normed = (centred * lax.rsqrt(spread + 1e-05) * gain_ref[...]).astype(jnp.bfloat16)
    for copy in copies[4:]:
        copy.wait()
    queries = jnp.dot(normed, wq_ref[...], preferred_element_type=jnp.float32).astype(jnp.bfloat16)
    lane = lax.broadcasted_iota(jnp.int32, (8, 128), 1)
    row = lax.broadcasted_iota(jnp.int32, (8, 128), 0)
    row_ref[:, 0:GROUP] = list_ref[...]
    entries = jnp.where(lane < GROUP, jnp.broadcast_to(row_ref[...], (8, 128)), 0)
    entries = jnp.where(lane == GROUP, jnp.broadcast_to(len_ref[...], (8, 128)), entries)
    dest = dest_ref[...]
    position = dest // (BLOCK * SECTORS) * 2 + dest % 2
    entries = jnp.where(row == 1, jnp.broadcast_to(position, (8, 128)), entries)
    head_lane = lax.broadcasted_iota(jnp.int32, (1, HEADS), 1)
    own = jnp.where(head_lane == lax.axis_index("y"), scale_ref[...], 0.0)
    own = jnp.broadcast_to(jnp.sum(own, axis=-1, keepdims=True), (8, 128))
    first = own.astype(jnp.bfloat16).astype(jnp.float32)
    second = (own - first).astype(jnp.bfloat16).astype(jnp.float32)
    parts = jnp.where(row == 2, first, jnp.where(row == 3, second, own - first - second))
    entries = jnp.where(row < 2, entries.astype(jnp.float32), parts).astype(jnp.bfloat16)
    low = low_lanes(HALF)
    sends = []
    for head in range(HEADS):
        tile = slice(head // 2 * 128, head // 2 * 128 + 128)
        keys = wkv_ref[:, tile]
        values = wkv_ref[:, slice(tile.start + 512, tile.stop + 512)]
        upper, lower = queries[0:HALF, tile], queries[HALF:BLOCK, tile]
        if head % 2:
            keys, upper = swap_halves(keys), swap_halves(upper)
        else:
            values, lower = swap_halves(values), swap_halves(lower)
        out_ref[head, 0:HALF] = lat_ref[...]
        out_ref[head, HALF:2 * HALF] = jnp.where(low, keys, values)
        out_ref[head, 2 * HALF:TAIL] = jnp.where(low, upper, lower)
        out_ref[head, TAIL:ROWS] = entries
        send = pltpu.make_async_copy(out_ref.at[head], out_hbm.at[head], out_sems.at[head])
        send.start()
        sends.append(send)
    for send in sends:
        send.wait()


def project_kernel(got_ref, out_ref, table_ref, position_ref, scale_ref):
    latent = got_ref[:, 0:HALF, :].reshape(SOURCES * HALF, 128)
    weights = got_ref[:, HALF:2 * HALF, :].reshape(SOURCES * HALF, 128)
    out_ref[...] = lax.dot_general(latent, weights, CONTRACT_FIRST, preferred_element_type=jnp.float32)
    lane = lax.broadcasted_iota(jnp.int32, (8, 128), 1)
    for source in range(SOURCES):
        row = got_ref[source, TAIL:ROWS, :].astype(jnp.float32).astype(jnp.int32)
        slots = jnp.bitwise_and(row, 1) * (GROUP // 2) + jnp.right_shift(row, 1)
        table_ref[source:source + 1] = jnp.where(lane == GROUP, row * BLOCK, slots)[0:1]
    own = got_ref[lax.axis_index("y"), TAIL:ROWS, :].astype(jnp.float32)
    position_ref[...] = own[1:2].astype(jnp.int32)
    scale_ref[...] = (own[2:3] + own[3:4]) + own[4:5]


def join_kernel(parts_ref, out_ref):
    panel = (parts_ref[0] + parts_ref[1]).astype(jnp.bfloat16)
    for peer in range(out_ref.shape[0]):
        out_ref[peer] = panel


def attend_kernel(table_ref, scale_ref, got_ref, panel_ref, out_ref, query_ref, score_ref, prob_ref, total_ref):
    scale = scale_ref[:, 0:1] * (math.log2(math.e) / math.sqrt(HEAD_DIM))
    low = low_lanes(HALF)
    for source in range(SOURCES):
        tile = got_ref[source, 2 * HALF:TAIL]
        zero = jnp.zeros_like(tile)
        query_ref[source * BLOCK:source * BLOCK + HALF] = jnp.where(low, tile, zero)
        query_ref[source * BLOCK + HALF:source * BLOCK + BLOCK] = jnp.where(low, swap_halves(tile), zero)

    def finish(source, weighted, denominator):
        attended = (weighted / denominator).astype(jnp.bfloat16)
        out_ref[source] = jnp.where(low, swap_halves(attended[0:HALF]), attended[HALF:BLOCK])

    def blocks_of(source):
        return jnp.concatenate([panel_ref[table_ref[source, j]] for j in range(LISTED)], axis=0)

    dense = table_ref[0, GROUP] > LISTED * BLOCK

    @pl.when(jnp.logical_not(dense))
    def _():
        for source in range(SOURCES):
            rows = slice(source * BLOCK, source * BLOCK + BLOCK)
            score = lax.dot_general(
                query_ref[rows], blocks_of(source), CONTRACT_LAST, preferred_element_type=jnp.float32
            )
            column = lax.broadcasted_iota(jnp.int32, score.shape, 1)
            score_ref[rows] = jnp.where(column < table_ref[source, GROUP], score, -jnp.inf)
        scores = score_ref[...]
        weights = jnp.exp2((scores - jnp.max(scores, axis=-1, keepdims=True)) * scale)
        total_ref[...] = jnp.broadcast_to(jnp.sum(weights, axis=-1, keepdims=True), total_ref.shape)
        prob_ref[...] = weights.astype(jnp.bfloat16)
        for source in range(SOURCES):
            rows = slice(source * BLOCK, source * BLOCK + BLOCK)
            weighted = jnp.dot(prob_ref[rows], blocks_of(source), preferred_element_type=jnp.float32)
            finish(source, weighted, total_ref[rows])

    @pl.when(dense)
    def _():
        keys = panel_ref[...].reshape(GROUP * BLOCK, 128)
        for first in range(0, SOURCES, PER_DOT):
            query = query_ref[first * BLOCK:(first + PER_DOT) * BLOCK]
            scores = lax.dot_general(query, keys, CONTRACT_LAST, preferred_element_type=jnp.float32)
            weights = jnp.exp2((scores - jnp.max(scores, axis=-1, keepdims=True)) * scale)
            total = jnp.sum(weights, axis=-1, keepdims=True)
            weighted = jnp.dot(weights.astype(jnp.bfloat16), keys, preferred_element_type=jnp.float32)
            for k in range(PER_DOT):
                rows = slice(k * BLOCK, k * BLOCK + BLOCK)
                finish(first + k, weighted[rows], total[rows])


def finish_kernel(got_ref, wo_ref, feat_ref, position_ref, out_ref):
    low = low_lanes(HALF)
    upper, lower = [], []
    for pair in range(HEADS // 2):
        even, odd = got_ref[2 * pair], got_ref[2 * pair + 1]
        upper.append(jnp.where(low, even, swap_halves(odd)))
        lower.append(jnp.where(low, swap_halves(even), odd))
    attended = jnp.concatenate([jnp.concatenate(upper, axis=1), jnp.concatenate(lower, axis=1)], axis=0)
    product = jnp.dot(attended, wo_ref[...], preferred_element_type=jnp.float32)
    updated = (feat_ref[...].astype(jnp.float32) + product).astype(jnp.bfloat16)
    slot = lax.broadcasted_iota(jnp.int32, (BLOCK, BLOCK), 0)
    chosen = (slot == position_ref[...]).astype(jnp.float32).astype(jnp.bfloat16)
    moved = jnp.dot(chosen, updated, preferred_element_type=jnp.float32)
    out_ref[...] = moved.reshape(out_ref.shape).astype(jnp.bfloat16)


def shards(grid_feat, latent, query_gain, w_q, w_kv, w_o, head_scale, block_lists, list_len, dest):
    local_rows, width = grid_feat.shape
    bf16, f32, i32 = jnp.bfloat16, jnp.float32, jnp.int32
    shaped = jax.ShapeDtypeStruct

    packed = pl.pallas_call(
        pack_kernel,
        out_shape=shaped((HEADS, ROWS, 128), bf16),
        in_specs=[HBM] * 9,
        out_specs=HBM,
        scratch_shapes=[
            pltpu.VMEM((local_rows, width), bf16),
            pltpu.VMEM((1, width), f32),
            pltpu.VMEM(latent.shape[::-1], bf16),
            pltpu.VMEM(w_kv.shape, bf16),
            pltpu.VMEM(w_q.shape, bf16),
            pltpu.VMEM((1, GROUP), i32),
            pltpu.VMEM((1, 1), i32),
            pltpu.VMEM((1, local_rows), i32),
            pltpu.VMEM((1, HEADS), f32),
            pltpu.VMEM((1, 128), i32),
            pltpu.VMEM((HEADS, ROWS, 128), bf16),
            pltpu.SemaphoreType.DMA((9,)),
            pltpu.SemaphoreType.DMA((HEADS,)),
        ],
        name="pack",
        compiler_params=pltpu.CompilerParams(vmem_limit_bytes=60 << 20),
    )(
        grid_feat, query_gain.reshape(1, -1), latent.T, w_kv, w_q, block_lists, list_len.reshape(1, 1),
        dest.reshape(1, -1), head_scale.reshape(1, -1),
    )
    got = lax.all_to_all(packed, "y", 0, 0, tiled=True)

    partial, table, position, scale = pl.pallas_call(
        project_kernel,
        out_shape=(
            shaped((BLOCK, 128), f32), shaped((SOURCES, 128), i32), shaped((1, 128), i32), shaped((1, 128), f32)
        ),
        in_specs=[VMEM],
        out_specs=(VMEM,) * 4,
        name="project",
        compiler_params=PARAMS,
    )(got)
    parts = lax.all_gather(partial, "xl", axis=0)
    panel = pl.pallas_call(
        join_kernel,
        out_shape=shaped((GROUP // 2, BLOCK, 128), bf16),
        in_specs=[VMEM],
        out_specs=VMEM,
        name="join",
        compiler_params=PARAMS,
    )(parts)
    panels = lax.all_to_all(panel, "z", 0, 0, tiled=True)
    panels = lax.all_gather(panels, "c", axis=0).reshape(GROUP, BLOCK, 128)

    attended = pl.pallas_call(
        attend_kernel,
        out_shape=shaped((SOURCES, HALF, 128), bf16),
        in_specs=[SMEM, VMEM, VMEM, VMEM],
        out_specs=VMEM,
        scratch_shapes=[
            pltpu.VMEM((SOURCES * BLOCK, 128), bf16),
            pltpu.VMEM((SOURCES * BLOCK, LISTED * BLOCK), f32),
            pltpu.VMEM((SOURCES * BLOCK, LISTED * BLOCK), bf16),
            pltpu.VMEM((SOURCES * BLOCK, 128), f32),
        ],
        name="attend",
        compiler_params=PARAMS,
    )(table, scale, got, panels)
    attended = lax.all_to_all(attended, "y", 0, 0, tiled=True)

    outgoing = pl.pallas_call(
        finish_kernel,
        out_shape=shaped((local_rows // 2, 2, width), bf16),
        in_specs=[VMEM] * 4,
        out_specs=VMEM,
        name="finish",
        compiler_params=PARAMS,
    )(attended, w_o, grid_feat, position)
    arrived = lax.all_to_all(outgoing, ("xh", "z", "c"), 0, 0, tiled=True)
    return arrived.reshape(local_rows, width)


def solution(mesh):
    fine = Mesh(mesh.devices.reshape(4, 8, 2, 2, 8), ("xh", "z", "c", "xl", "y"))
    band, sector = ("xh", "z", "c"), ("xl", "y")
    return jax.shard_map(
        shards,
        mesh=fine,
        in_specs=(
            P(band + sector, None),
            P(band, sector),
            P(),
            P(),
            P(sector, None),
            P(),
            P(),
            P(band + sector, None),
            P(band + sector),
            P(band + sector),
        ),
        out_specs=P(band + sector, None),
        check_vma=False,
    )
```

```python
import math

import jax
import jax.numpy as jnp
from jax import lax
from jax.experimental import pallas as pl
from jax.experimental.pallas import tpu as pltpu
from jax.sharding import Mesh, PartitionSpec as P

HEADS = 8
BLOCK = 128
HEAD_DIM = 64
HALF = 64
LISTED = 4
GROUP = 16
SECTORS = 16
SOURCES = 8
ROWS = 200
TAIL = 3 * HALF
PER_DOT = 4

VMEM = pl.BlockSpec(memory_space=pltpu.VMEM)
SMEM = pl.BlockSpec(memory_space=pltpu.SMEM)
HBM = pl.BlockSpec(memory_space=pltpu.HBM)
PARAMS = pltpu.CompilerParams(vmem_limit_bytes=24 << 20)
CONTRACT_LAST = (((1,), (1,)), ((), ()))
CONTRACT_FIRST = (((0,), (0,)), ((), ()))


def low_lanes(rows):
    return lax.broadcasted_iota(jnp.int32, (rows, 128), 1) < HALF


def swap_halves(x):
    return jnp.concatenate([x[:, HALF:], x[:, :HALF]], axis=1)


def pack_kernel(
    feat_hbm, gain_hbm, lat_hbm, wkv_hbm, wq_hbm, list_hbm, len_hbm, dest_hbm, scale_hbm, out_ref,
    feat_ref, gain_ref, lat_ref, wkv_ref, wq_ref, list_ref, len_ref, dest_ref, scale_ref, row_ref, sems,
):
    pairs = (
        (feat_hbm, feat_ref), (gain_hbm, gain_ref), (lat_hbm, lat_ref), (wkv_hbm, wkv_ref),
        (wq_hbm, wq_ref), (list_hbm, list_ref), (len_hbm, len_ref), (dest_hbm, dest_ref), (scale_hbm, scale_ref),
    )
    copies = [pltpu.make_async_copy(source, target, sems.at[k]) for k, (source, target) in enumerate(pairs)]
    for copy in copies:
        copy.start()
    for copy in copies[:4]:
        copy.wait()
    values = feat_ref[...].astype(jnp.float32)
    centred = values - jnp.mean(values, axis=-1, keepdims=True)
    spread = jnp.mean(centred * centred, axis=-1, keepdims=True)
    normed = (centred * lax.rsqrt(spread + 1e-05) * gain_ref[...]).astype(jnp.bfloat16)
    for copy in copies[4:]:
        copy.wait()
    queries = jnp.dot(normed, wq_ref[...], preferred_element_type=jnp.float32).astype(jnp.bfloat16)
    lane = lax.broadcasted_iota(jnp.int32, (8, 128), 1)
    row = lax.broadcasted_iota(jnp.int32, (8, 128), 0)
    row_ref[:, 0:GROUP] = list_ref[...]
    entries = jnp.where(lane < GROUP, jnp.broadcast_to(row_ref[...], (8, 128)), 0)
    entries = jnp.where(lane == GROUP, jnp.broadcast_to(len_ref[...], (8, 128)), entries)
    dest = dest_ref[...]
    position = dest // (BLOCK * SECTORS) * 2 + dest % 2
    entries = jnp.where(row == 1, jnp.broadcast_to(position, (8, 128)), entries)
    head_lane = lax.broadcasted_iota(jnp.int32, (1, HEADS), 1)
    own = jnp.where(head_lane == lax.axis_index("y"), scale_ref[...], 0.0)
    own = jnp.broadcast_to(jnp.sum(own, axis=-1, keepdims=True), (8, 128))
    first = own.astype(jnp.bfloat16).astype(jnp.float32)
    second = (own - first).astype(jnp.bfloat16).astype(jnp.float32)
    parts = jnp.where(row == 2, first, jnp.where(row == 3, second, own - first - second))
    entries = jnp.where(row < 2, entries.astype(jnp.float32), parts).astype(jnp.bfloat16)
    low = low_lanes(HALF)
    for head in range(HEADS):
        tile = slice(head // 2 * 128, head // 2 * 128 + 128)
        keys = wkv_ref[:, tile]
        values = wkv_ref[:, slice(tile.start + 512, tile.stop + 512)]
        upper, lower = queries[0:HALF, tile], queries[HALF:BLOCK, tile]
        if head % 2:
            keys, upper = swap_halves(keys), swap_halves(upper)
        else:
            values, lower = swap_halves(values), swap_halves(lower)
        out_ref[head, 0:HALF] = lat_ref[...]
        out_ref[head, HALF:2 * HALF] = jnp.where(low, keys, values)
        out_ref[head, 2 * HALF:TAIL] = jnp.where(low, upper, lower)
        out_ref[head, TAIL:ROWS] = entries


def project_kernel(got_ref, out_ref, table_ref, position_ref, scale_ref):
    latent = got_ref[:, 0:HALF, :].reshape(SOURCES * HALF, 128)
    weights = got_ref[:, HALF:2 * HALF, :].reshape(SOURCES * HALF, 128)
    out_ref[...] = lax.dot_general(latent, weights, CONTRACT_FIRST, preferred_element_type=jnp.float32)
    lane = lax.broadcasted_iota(jnp.int32, (8, 128), 1)
    for source in range(SOURCES):
        row = got_ref[source, TAIL:ROWS, :].astype(jnp.float32).astype(jnp.int32)
        slots = jnp.bitwise_and(row, 1) * (GROUP // 2) + jnp.right_shift(row, 1)
        table_ref[source:source + 1] = jnp.where(lane == GROUP, row * BLOCK, slots)[0:1]
    own = got_ref[lax.axis_index("y"), TAIL:ROWS, :].astype(jnp.float32)
    position_ref[...] = own[1:2].astype(jnp.int32)
    scale_ref[...] = (own[2:3] + own[3:4]) + own[4:5]


def join_kernel(parts_ref, out_ref):
    panel = (parts_ref[0] + parts_ref[1]).astype(jnp.bfloat16)
    for peer in range(out_ref.shape[0]):
        out_ref[peer] = panel


def attend_kernel(table_ref, scale_ref, got_ref, panel_ref, out_ref, query_ref, score_ref, prob_ref, total_ref, values_ref, full_ref):
    scale = scale_ref[:, 0:1] * (math.log2(math.e) / math.sqrt(HEAD_DIM))
    low = low_lanes(HALF)
    for source in range(SOURCES):
        tile = got_ref[source, 2 * HALF:TAIL]
        zero = jnp.zeros_like(tile)
        query_ref[source * BLOCK:source * BLOCK + HALF] = jnp.where(low, tile, zero)
        query_ref[source * BLOCK + HALF:source * BLOCK + BLOCK] = jnp.where(low, swap_halves(tile), zero)

    def finish(source, weighted, denominator):
        attended = (weighted / denominator).astype(jnp.bfloat16)
        out_ref[source] = jnp.where(low, swap_halves(attended[0:HALF]), attended[HALF:BLOCK])

    def blocks_of(source):
        return jnp.concatenate([panel_ref[table_ref[source, j]] for j in range(LISTED)], axis=0)

    dense = table_ref[0, GROUP] > LISTED * BLOCK

    @pl.when(jnp.logical_not(dense))
    def _():
        for source in range(SOURCES):
            rows = slice(source * BLOCK, source * BLOCK + BLOCK)
            score = lax.dot_general(
                query_ref[rows], blocks_of(source), CONTRACT_LAST, preferred_element_type=jnp.float32
            )
            column = lax.broadcasted_iota(jnp.int32, score.shape, 1)
            score_ref[rows] = jnp.where(column < table_ref[source, GROUP], score, -jnp.inf)
        scores = score_ref[...]
        weights = jnp.exp2((scores - jnp.max(scores, axis=-1, keepdims=True)) * scale)
        total_ref[...] = jnp.broadcast_to(jnp.sum(weights, axis=-1, keepdims=True), total_ref.shape)
        prob_ref[...] = weights.astype(jnp.bfloat16)
        for source in range(SOURCES):
            rows = slice(source * BLOCK, source * BLOCK + BLOCK)
            weighted = jnp.dot(prob_ref[rows], blocks_of(source), preferred_element_type=jnp.float32)
            finish(source, weighted, total_ref[rows])

    @pl.when(dense)
    def _():
        keys = panel_ref[...].reshape(GROUP * BLOCK, 128)
        span = PER_DOT * BLOCK

        def score(first):
            query = query_ref[first * BLOCK:first * BLOCK + span]
            full_ref[:, first * BLOCK:first * BLOCK + span] = lax.dot_general(
                keys, query, CONTRACT_LAST, preferred_element_type=jnp.float32
            )

        def rest(first):
            scores = full_ref[:, first * BLOCK:first * BLOCK + span]
            weights = jnp.exp2((scores - jnp.max(scores, axis=0, keepdims=True)) * scale)
            total = jnp.sum(weights, axis=0, keepdims=True)
            weighted = jnp.dot(values_ref[...], weights.astype(jnp.bfloat16), preferred_element_type=jnp.float32)
            attended = weighted / total
            for k in range(PER_DOT):
                piece = attended[:, k * BLOCK:k * BLOCK + BLOCK]
                piece = jnp.transpose(jnp.concatenate([piece, swap_halves(piece)], axis=0))
                out_ref[first + k] = piece[0:HALF].astype(jnp.bfloat16)

        score(0)
        for block in range(GROUP):
            turned = jnp.transpose(panel_ref[block].astype(jnp.float32))
            values_ref[:, block * BLOCK:block * BLOCK + BLOCK] = turned[HALF:BLOCK].astype(jnp.bfloat16)
        for first in range(0, SOURCES, PER_DOT):
            if first + PER_DOT < SOURCES:
                score(first + PER_DOT)
            rest(first)


def finish_kernel(got_ref, wo_ref, feat_ref, position_ref, out_ref):
    low = low_lanes(HALF)
    upper, lower = [], []
    for pair in range(HEADS // 2):
        even, odd = got_ref[2 * pair], got_ref[2 * pair + 1]
        upper.append(jnp.where(low, even, swap_halves(odd)))
        lower.append(jnp.where(low, swap_halves(even), odd))
    attended = jnp.concatenate([jnp.concatenate(upper, axis=1), jnp.concatenate(lower, axis=1)], axis=0)
    product = jnp.dot(attended, wo_ref[...], preferred_element_type=jnp.float32)
    updated = (feat_ref[...].astype(jnp.float32) + product).astype(jnp.bfloat16)
    slot = lax.broadcasted_iota(jnp.int32, (BLOCK, BLOCK), 0)
    chosen = (slot == position_ref[...]).astype(jnp.float32).astype(jnp.bfloat16)
    moved = jnp.dot(chosen, updated, preferred_element_type=jnp.float32)
    out_ref[...] = moved.reshape(out_ref.shape).astype(jnp.bfloat16)


def shards(grid_feat, latent, query_gain, w_q, w_kv, w_o, head_scale, block_lists, list_len, dest):
    local_rows, width = grid_feat.shape
    bf16, f32, i32 = jnp.bfloat16, jnp.float32, jnp.int32
    shaped = jax.ShapeDtypeStruct

    packed = pl.pallas_call(
        pack_kernel,
        out_shape=shaped((HEADS, ROWS, 128), bf16),
        in_specs=[HBM] * 9,
        out_specs=VMEM,
        scratch_shapes=[
            pltpu.VMEM((local_rows, width), bf16),
            pltpu.VMEM((1, width), f32),
            pltpu.VMEM(latent.shape[::-1], bf16),
            pltpu.VMEM(w_kv.shape, bf16),
            pltpu.VMEM(w_q.shape, bf16),
            pltpu.VMEM((1, GROUP), i32),
            pltpu.VMEM((1, 1), i32),
            pltpu.VMEM((1, local_rows), i32),
            pltpu.VMEM((1, HEADS), f32),
            pltpu.VMEM((1, 128), i32),
            pltpu.SemaphoreType.DMA((9,)),
        ],
        name="pack",
        compiler_params=pltpu.CompilerParams(vmem_limit_bytes=12 << 20),
    )(
        *(
            pltpu.with_memory_space_constraint(x, pltpu.HBM)
            for x in (grid_feat, query_gain.reshape(1, -1), latent.T, w_kv, w_q, block_lists)
        ),
        list_len.reshape(1, 1),
        pltpu.with_memory_space_constraint(dest.reshape(1, -1), pltpu.HBM),
        pltpu.with_memory_space_constraint(head_scale.reshape(1, -1), pltpu.HBM),
    )
    got = lax.all_to_all(packed, "y", 0, 0, tiled=True)

    partial, table, position, scale = pl.pallas_call(
        project_kernel,
        out_shape=(
            shaped((BLOCK, 128), f32), shaped((SOURCES, 128), i32), shaped((1, 128), i32), shaped((1, 128), f32)
        ),
        in_specs=[VMEM],
        out_specs=(VMEM,) * 4,
        name="project",
        compiler_params=PARAMS,
    )(got)
    parts = lax.all_gather(partial, "xl", axis=0)
    panel = pl.pallas_call(
        join_kernel,
        out_shape=shaped((GROUP // 2, BLOCK, 128), bf16),
        in_specs=[VMEM],
        out_specs=VMEM,
        name="join",
        compiler_params=PARAMS,
    )(parts)
    panels = lax.all_to_all(panel, "z", 0, 0, tiled=True)
    panels = lax.all_gather(panels, "c", axis=0).reshape(GROUP, BLOCK, 128)

    attended = pl.pallas_call(
        attend_kernel,
        out_shape=shaped((SOURCES, HALF, 128), bf16),
        in_specs=[SMEM, VMEM, VMEM, VMEM],
        out_specs=VMEM,
        scratch_shapes=[
            pltpu.VMEM((SOURCES * BLOCK, 128), bf16),
            pltpu.VMEM((SOURCES * BLOCK, LISTED * BLOCK), f32),
            pltpu.VMEM((SOURCES * BLOCK, LISTED * BLOCK), bf16),
            pltpu.VMEM((SOURCES * BLOCK, 128), f32),
            pltpu.VMEM((HALF, GROUP * BLOCK), bf16),
            pltpu.VMEM((GROUP * BLOCK, SOURCES * BLOCK), f32),
        ],
        name="attend",
        compiler_params=PARAMS,
    )(table, scale, got, panels)
    attended = lax.all_to_all(attended, "y", 0, 0, tiled=True)

    outgoing = pl.pallas_call(
        finish_kernel,
        out_shape=shaped((local_rows // 2, 2, width), bf16),
        in_specs=[VMEM] * 4,
        out_specs=VMEM,
        name="finish",
        compiler_params=PARAMS,
    )(attended, w_o, grid_feat, position)
    arrived = lax.all_to_all(outgoing, ("xh", "z", "c"), 0, 0, tiled=True)
    return arrived.reshape(local_rows, width)


def solution(mesh):
    fine = Mesh(mesh.devices.reshape(4, 8, 2, 2, 8), ("xh", "z", "c", "xl", "y"))
    band, sector = ("xh", "z", "c"), ("xl", "y")
    return jax.shard_map(
        shards,
        mesh=fine,
        in_specs=(
            P(band + sector, None),
            P(band, sector),
            P(),
            P(),
            P(sector, None),
            P(),
            P(),
            P(band + sector, None),
            P(band + sector),
            P(band + sector),
        ),
        out_specs=P(band + sector, None),
        check_vma=False,
    )
```

```python
import math

import jax
import jax.numpy as jnp
from jax import lax
from jax.experimental import pallas as pl
from jax.experimental.pallas import tpu as pltpu
from jax.sharding import Mesh, PartitionSpec as P

HEADS = 8
BLOCK = 128
HEAD_DIM = 64
HALF = 64
LISTED = 4
GROUP = 16
SECTORS = 16
SOURCES = 8
ROWS = 200
TAIL = 3 * HALF
PER_DOT = 4

VMEM = pl.BlockSpec(memory_space=pltpu.VMEM)
ANY = pl.BlockSpec(memory_space=pl.ANY)
HBM = pl.BlockSpec(memory_space=pltpu.HBM)
PARAMS = pltpu.CompilerParams(vmem_limit_bytes=24 << 20)
CONTRACT_LAST = (((1,), (1,)), ((), ()))
CONTRACT_FIRST = (((0,), (0,)), ((), ()))


def low_lanes(rows):
    return lax.broadcasted_iota(jnp.int32, (rows, 128), 1) < HALF


def swap_halves(x):
    return jnp.concatenate([x[:, HALF:], x[:, :HALF]], axis=1)


def pack_kernel(
    feat_hbm, gain_hbm, lat_hbm, wkv_hbm, wq_hbm, list_hbm, len_hbm, dest_hbm, scale_hbm, out_ref,
    feat_ref, gain_ref, lat_ref, wkv_ref, wq_ref, list_ref, len_ref, dest_ref, scale_ref, row_ref, sems,
):
    pairs = (
        (feat_hbm, feat_ref), (gain_hbm, gain_ref), (lat_hbm, lat_ref), (wkv_hbm, wkv_ref),
        (wq_hbm, wq_ref), (list_hbm, list_ref), (len_hbm, len_ref), (dest_hbm, dest_ref), (scale_hbm, scale_ref),
    )
    copies = [pltpu.make_async_copy(source, target, sems.at[k]) for k, (source, target) in enumerate(pairs)]
    for copy in copies:
        copy.start()
    for copy in copies[:4]:
        copy.wait()
    values = feat_ref[...].astype(jnp.float32)
    centred = values - jnp.mean(values, axis=-1, keepdims=True)
    spread = jnp.mean(centred * centred, axis=-1, keepdims=True)
    normed = (centred * lax.rsqrt(spread + 1e-05) * gain_ref[...]).astype(jnp.bfloat16)
    low = low_lanes(HALF)
    for head in range(HEADS):
        tile = slice(head // 2 * 128, head // 2 * 128 + 128)
        keys = wkv_ref[:, tile]
        values = wkv_ref[:, slice(tile.start + 512, tile.stop + 512)]
        if head % 2:
            keys = swap_halves(keys)
        else:
            values = swap_halves(values)
        out_ref[head, 0:HALF] = lat_ref[...]
        out_ref[head, HALF:2 * HALF] = jnp.where(low, keys, values)
    for copy in copies[4:]:
        copy.wait()
    queries = jnp.dot(normed, wq_ref[...], preferred_element_type=jnp.float32).astype(jnp.bfloat16)
    lane = lax.broadcasted_iota(jnp.int32, (8, 128), 1)
    row = lax.broadcasted_iota(jnp.int32, (8, 128), 0)
    row_ref[:, 0:GROUP] = list_ref[...]
    entries = jnp.where(lane < GROUP, jnp.broadcast_to(row_ref[...], (8, 128)), 0)
    entries = jnp.where(lane == GROUP, jnp.broadcast_to(len_ref[...], (8, 128)), entries)
    dest = dest_ref[...]
    position = dest // (BLOCK * SECTORS) * 2 + dest % 2
    entries = jnp.where(row == 1, jnp.broadcast_to(position, (8, 128)), entries)
    head_lane = lax.broadcasted_iota(jnp.int32, (1, HEADS), 1)
    own = jnp.where(head_lane == lax.axis_index("y"), scale_ref[...], 0.0)
    own = jnp.broadcast_to(jnp.sum(own, axis=-1, keepdims=True), (8, 128))
    first = own.astype(jnp.bfloat16).astype(jnp.float32)
    second = (own - first).astype(jnp.bfloat16).astype(jnp.float32)
    parts = jnp.where(row == 2, first, jnp.where(row == 3, second, own - first - second))
    entries = jnp.where(row < 2, entries.astype(jnp.float32), parts).astype(jnp.bfloat16)
    for head in range(HEADS):
        tile = slice(head // 2 * 128, head // 2 * 128 + 128)
        upper, lower = queries[0:HALF, tile], queries[HALF:BLOCK, tile]
        if head % 2:
            upper = swap_halves(upper)
        else:
            lower = swap_halves(lower)
        out_ref[head, 2 * HALF:TAIL] = jnp.where(low, upper, lower)
        out_ref[head, TAIL:ROWS] = entries


def project_kernel(got_ref, out_ref, table_ref, position_ref, scale_ref):
    latent = got_ref[:, 0:HALF, :].reshape(SOURCES * HALF, 128)
    weights = got_ref[:, HALF:2 * HALF, :].reshape(SOURCES * HALF, 128)
    out_ref[...] = lax.dot_general(latent, weights, CONTRACT_FIRST, preferred_element_type=jnp.float32)
    lane = lax.broadcasted_iota(jnp.int32, (8, 128), 1)
    for source in range(SOURCES):
        row = got_ref[source, TAIL:ROWS, :].astype(jnp.float32).astype(jnp.int32)
        slots = jnp.bitwise_and(row, 1) * (GROUP // 2) + jnp.right_shift(row, 1)
        table_ref[source:source + 1] = jnp.where(lane == GROUP, row * BLOCK, slots)[0:1]
    own = got_ref[lax.axis_index("y"), TAIL:ROWS, :].astype(jnp.float32)
    position_ref[...] = own[1:2].astype(jnp.int32)
    scale_ref[...] = (own[2:3] + own[3:4]) + own[4:5]


def join_kernel(parts_ref, out_ref):
    panel = (parts_ref[0] + parts_ref[1]).astype(jnp.bfloat16)
    for peer in range(out_ref.shape[0]):
        out_ref[peer] = panel


def attend_kernel(
    table_any, scale_ref, got_ref, panel_ref, out_ref,
    query_ref, score_ref, prob_ref, total_ref, values_ref, full_ref, table_ref, sem,
):
    fetch = pltpu.make_async_copy(table_any, table_ref, sem)
    fetch.start()
    scale = scale_ref[:, 0:1] * (math.log2(math.e) / math.sqrt(HEAD_DIM))
    low = low_lanes(HALF)
    for source in range(SOURCES):
        tile = got_ref[source, 2 * HALF:TAIL]
        zero = jnp.zeros_like(tile)
        query_ref[source * BLOCK:source * BLOCK + HALF] = jnp.where(low, tile, zero)
        query_ref[source * BLOCK + HALF:source * BLOCK + BLOCK] = jnp.where(low, swap_halves(tile), zero)

    def finish(source, weighted, denominator):
        attended = (weighted / denominator).astype(jnp.bfloat16)
        out_ref[source] = jnp.where(low, swap_halves(attended[0:HALF]), attended[HALF:BLOCK])

    def blocks_of(source):
        return jnp.concatenate([panel_ref[table_ref[source, j]] for j in range(LISTED)], axis=0)

    fetch.wait()
    dense = table_ref[0, GROUP] > LISTED * BLOCK

    @pl.when(jnp.logical_not(dense))
    def _():
        for source in range(SOURCES):
            rows = slice(source * BLOCK, source * BLOCK + BLOCK)
            score = lax.dot_general(
                query_ref[rows], blocks_of(source), CONTRACT_LAST, preferred_element_type=jnp.float32
            )
            column = lax.broadcasted_iota(jnp.int32, score.shape, 1)
            score_ref[rows] = jnp.where(column < table_ref[source, GROUP], score, -jnp.inf)
        scores = score_ref[...]
        weights = jnp.exp2((scores - jnp.max(scores, axis=-1, keepdims=True)) * scale)
        total_ref[...] = jnp.broadcast_to(jnp.sum(weights, axis=-1, keepdims=True), total_ref.shape)
        prob_ref[...] = weights.astype(jnp.bfloat16)
        for source in range(SOURCES):
            rows = slice(source * BLOCK, source * BLOCK + BLOCK)
            weighted = jnp.dot(prob_ref[rows], blocks_of(source), preferred_element_type=jnp.float32)
            finish(source, weighted, total_ref[rows])

    @pl.when(dense)
    def _():
        keys = panel_ref[...].reshape(GROUP * BLOCK, 128)
        span = PER_DOT * BLOCK

        def score(first):
            query = query_ref[first * BLOCK:first * BLOCK + span]
            full_ref[:, first * BLOCK:first * BLOCK + span] = lax.dot_general(
                keys, query, CONTRACT_LAST, preferred_element_type=jnp.float32
            )

        def rest(first):
            scores = full_ref[:, first * BLOCK:first * BLOCK + span]
            weights = jnp.exp2((scores - jnp.max(scores, axis=0, keepdims=True)) * scale)
            total = jnp.sum(weights, axis=0, keepdims=True)
            weighted = jnp.dot(values_ref[...], weights.astype(jnp.bfloat16), preferred_element_type=jnp.float32)
            attended = weighted / total
            for k in range(PER_DOT):
                piece = attended[:, k * BLOCK:k * BLOCK + BLOCK]
                piece = jnp.transpose(jnp.concatenate([piece, swap_halves(piece)], axis=0))
                out_ref[first + k] = piece[0:HALF].astype(jnp.bfloat16)

        score(0)
        for block in range(GROUP):
            turned = jnp.transpose(panel_ref[block].astype(jnp.float32))
            values_ref[:, block * BLOCK:block * BLOCK + BLOCK] = turned[HALF:BLOCK].astype(jnp.bfloat16)
        for first in range(0, SOURCES, PER_DOT):
            if first + PER_DOT < SOURCES:
                score(first + PER_DOT)
            rest(first)


def finish_kernel(got_ref, wo_ref, feat_ref, position_ref, out_ref):
    low = low_lanes(HALF)
    upper, lower = [], []
    for pair in range(HEADS // 2):
        even, odd = got_ref[2 * pair], got_ref[2 * pair + 1]
        upper.append(jnp.where(low, even, swap_halves(odd)))
        lower.append(jnp.where(low, swap_halves(even), odd))
    attended = jnp.concatenate([jnp.concatenate(upper, axis=1), jnp.concatenate(lower, axis=1)], axis=0)
    product = jnp.dot(attended, wo_ref[...], preferred_element_type=jnp.float32)
    updated = (feat_ref[...].astype(jnp.float32) + product).astype(jnp.bfloat16)
    slot = lax.broadcasted_iota(jnp.int32, (BLOCK, BLOCK), 0)
    chosen = (slot == position_ref[...]).astype(jnp.float32).astype(jnp.bfloat16)
    moved = jnp.dot(chosen, updated, preferred_element_type=jnp.float32)
    out_ref[...] = moved.reshape(out_ref.shape).astype(jnp.bfloat16)


def shards(grid_feat, latent, query_gain, w_q, w_kv, w_o, head_scale, block_lists, list_len, dest):
    local_rows, width = grid_feat.shape
    bf16, f32, i32 = jnp.bfloat16, jnp.float32, jnp.int32
    shaped = jax.ShapeDtypeStruct

    packed = pl.pallas_call(
        pack_kernel,
        out_shape=shaped((HEADS, ROWS, 128), bf16),
        in_specs=[HBM] * 9,
        out_specs=VMEM,
        scratch_shapes=[
            pltpu.VMEM((local_rows, width), bf16),
            pltpu.VMEM((1, width), f32),
            pltpu.VMEM(latent.shape[::-1], bf16),
            pltpu.VMEM(w_kv.shape, bf16),
            pltpu.VMEM(w_q.shape, bf16),
            pltpu.VMEM((1, GROUP), i32),
            pltpu.VMEM((1, 1), i32),
            pltpu.VMEM((1, local_rows), i32),
            pltpu.VMEM((1, HEADS), f32),
            pltpu.VMEM((1, 128), i32),
            pltpu.SemaphoreType.DMA((9,)),
        ],
        name="pack",
        compiler_params=pltpu.CompilerParams(vmem_limit_bytes=12 << 20),
    )(
        *(
            pltpu.with_memory_space_constraint(x, pltpu.HBM)
            for x in (grid_feat, query_gain.reshape(1, -1), latent.T, w_kv, w_q, block_lists)
        ),
        list_len.reshape(1, 1),
        pltpu.with_memory_space_constraint(dest.reshape(1, -1), pltpu.HBM),
        pltpu.with_memory_space_constraint(head_scale.reshape(1, -1), pltpu.HBM),
    )
    got = lax.all_to_all(packed, "y", 0, 0, tiled=True)

    partial, table, position, scale = pl.pallas_call(
        project_kernel,
        out_shape=(
            shaped((BLOCK, 128), f32), shaped((SOURCES, 128), i32), shaped((1, 128), i32), shaped((1, 128), f32)
        ),
        in_specs=[VMEM],
        out_specs=(VMEM,) * 4,
        name="project",
        compiler_params=PARAMS,
    )(got)
    parts = lax.all_gather(partial, "xl", axis=0)
    panel = pl.pallas_call(
        join_kernel,
        out_shape=shaped((GROUP // 2, BLOCK, 128), bf16),
        in_specs=[VMEM],
        out_specs=VMEM,
        name="join",
        compiler_params=PARAMS,
    )(parts)
    panels = lax.all_to_all(panel, "z", 0, 0, tiled=True)
    panels = lax.all_gather(panels, "c", axis=0).reshape(GROUP, BLOCK, 128)

    attended = pl.pallas_call(
        attend_kernel,
        out_shape=shaped((SOURCES, HALF, 128), bf16),
        in_specs=[ANY, VMEM, VMEM, VMEM],
        out_specs=VMEM,
        scratch_shapes=[
            pltpu.VMEM((SOURCES * BLOCK, 128), bf16),
            pltpu.VMEM((SOURCES * BLOCK, LISTED * BLOCK), f32),
            pltpu.VMEM((SOURCES * BLOCK, LISTED * BLOCK), bf16),
            pltpu.VMEM((SOURCES * BLOCK, 128), f32),
            pltpu.VMEM((HALF, GROUP * BLOCK), bf16),
            pltpu.VMEM((GROUP * BLOCK, SOURCES * BLOCK), f32),
            pltpu.SMEM((SOURCES, 128), i32),
            pltpu.SemaphoreType.DMA,
        ],
        name="attend",
        compiler_params=PARAMS,
    )(table, scale, got, panels)
    attended = lax.all_to_all(attended, "y", 0, 0, tiled=True)

    outgoing = pl.pallas_call(
        finish_kernel,
        out_shape=shaped((local_rows // 2, 2, width), bf16),
        in_specs=[VMEM] * 4,
        out_specs=VMEM,
        name="finish",
        compiler_params=PARAMS,
    )(attended, w_o, grid_feat, position)
    arrived = lax.all_to_all(outgoing, ("xh", "z", "c"), 0, 0, tiled=True)
    return arrived.reshape(local_rows, width)


def solution(mesh):
    fine = Mesh(mesh.devices.reshape(4, 8, 2, 2, 8), ("xh", "z", "c", "xl", "y"))
    band, sector = ("xh", "z", "c"), ("xl", "y")
    return jax.shard_map(
        shards,
        mesh=fine,
        in_specs=(
            P(band + sector, None),
            P(band, sector),
            P(),
            P(),
            P(sector, None),
            P(),
            P(),
            P(band + sector, None),
            P(band + sector),
            P(band + sector),
        ),
        out_specs=P(band + sector, None),
        check_vma=False,
    )
```

```python
import math

import jax
import jax.numpy as jnp
from jax import lax
from jax.experimental import pallas as pl
from jax.experimental.pallas import tpu as pltpu
from jax.sharding import Mesh, PartitionSpec as P

HEADS = 8
BLOCK = 128
HEAD_DIM = 64
HALF = 64
LISTED = 4
GROUP = 16
SECTORS = 16
SOURCES = 8
ROWS = 200
TAIL = 3 * HALF
PER_DOT = 4
CHUNK = 16

VMEM = pl.BlockSpec(memory_space=pltpu.VMEM)
ANY = pl.BlockSpec(memory_space=pl.ANY)
HBM = pl.BlockSpec(memory_space=pltpu.HBM)
PARAMS = pltpu.CompilerParams(vmem_limit_bytes=24 << 20)
CONTRACT_LAST = (((1,), (1,)), ((), ()))
CONTRACT_FIRST = (((0,), (0,)), ((), ()))


def low_lanes(rows):
    return lax.broadcasted_iota(jnp.int32, (rows, 128), 1) < HALF


def swap_halves(x):
    return jnp.concatenate([x[:, HALF:], x[:, :HALF]], axis=1)


def pack_kernel(
    feat_hbm, gain_hbm, lat_hbm, wkv_hbm, wq_hbm, list_hbm, len_hbm, dest_hbm, scale_hbm, out_ref,
    feat_ref, gain_ref, lat_ref, wkv_ref, wq_ref, list_ref, len_ref, dest_ref, scale_ref, row_ref, sems,
):
    pairs = (
        (feat_hbm, feat_ref), (gain_hbm, gain_ref), (lat_hbm, lat_ref), (wkv_hbm, wkv_ref),
        (wq_hbm, wq_ref), (list_hbm, list_ref), (len_hbm, len_ref), (dest_hbm, dest_ref), (scale_hbm, scale_ref),
    )
    copies = [pltpu.make_async_copy(source, target, sems.at[k]) for k, (source, target) in enumerate(pairs)]
    for copy in copies:
        copy.start()
    for copy in copies[:4]:
        copy.wait()
    values = feat_ref[...].astype(jnp.float32)
    centred = values - jnp.mean(values, axis=-1, keepdims=True)
    spread = jnp.mean(centred * centred, axis=-1, keepdims=True)
    normed = (centred * lax.rsqrt(spread + 1e-05) * gain_ref[...]).astype(jnp.bfloat16)
    low = low_lanes(HALF)
    for head in range(HEADS):
        tile = slice(head // 2 * 128, head // 2 * 128 + 128)
        keys = wkv_ref[:, tile]
        values = wkv_ref[:, slice(tile.start + 512, tile.stop + 512)]
        if head % 2:
            keys = swap_halves(keys)
        else:
            values = swap_halves(values)
        out_ref[head, 0:HALF] = lat_ref[...]
        out_ref[head, HALF:2 * HALF] = jnp.where(low, keys, values)
    for copy in copies[4:]:
        copy.wait()
    queries = jnp.dot(normed, wq_ref[...], preferred_element_type=jnp.float32).astype(jnp.bfloat16)
    lane = lax.broadcasted_iota(jnp.int32, (8, 128), 1)
    row = lax.broadcasted_iota(jnp.int32, (8, 128), 0)
    row_ref[:, 0:GROUP] = list_ref[...]
    entries = jnp.where(lane < GROUP, jnp.broadcast_to(row_ref[...], (8, 128)), 0)
    entries = jnp.where(lane == GROUP, jnp.broadcast_to(len_ref[...], (8, 128)), entries)
    dest = dest_ref[...]
    position = dest // (BLOCK * SECTORS) * 2 + dest % 2
    entries = jnp.where(row == 1, jnp.broadcast_to(position, (8, 128)), entries)
    head_lane = lax.broadcasted_iota(jnp.int32, (1, HEADS), 1)
    own = jnp.where(head_lane == lax.axis_index("y"), scale_ref[...], 0.0)
    own = jnp.broadcast_to(jnp.sum(own, axis=-1, keepdims=True), (8, 128))
    first = own.astype(jnp.bfloat16).astype(jnp.float32)
    second = (own - first).astype(jnp.bfloat16).astype(jnp.float32)
    parts = jnp.where(row == 2, first, jnp.where(row == 3, second, own - first - second))
    entries = jnp.where(row < 2, entries.astype(jnp.float32), parts).astype(jnp.bfloat16)
    for head in range(HEADS):
        tile = slice(head // 2 * 128, head // 2 * 128 + 128)
        upper, lower = queries[0:HALF, tile], queries[HALF:BLOCK, tile]
        if head % 2:
            upper = swap_halves(upper)
        else:
            lower = swap_halves(lower)
        out_ref[head, 2 * HALF:TAIL] = jnp.where(low, upper, lower)
        out_ref[head, TAIL:ROWS] = entries


def project_kernel(got_ref, out_ref, table_ref, position_ref, scale_ref):
    latent = got_ref[:, 0:HALF, :].reshape(SOURCES * HALF, 128)
    weights = got_ref[:, HALF:2 * HALF, :].reshape(SOURCES * HALF, 128)
    out_ref[...] = lax.dot_general(latent, weights, CONTRACT_FIRST, preferred_element_type=jnp.float32)
    lane = lax.broadcasted_iota(jnp.int32, (8, 128), 1)
    for source in range(SOURCES):
        row = got_ref[source, TAIL:ROWS, :].astype(jnp.float32).astype(jnp.int32)
        slots = jnp.bitwise_and(row, 1) * (GROUP // 2) + jnp.right_shift(row, 1)
        table_ref[source:source + 1] = jnp.where(lane == GROUP, row * BLOCK, slots)[0:1]
    own = got_ref[lax.axis_index("y"), TAIL:ROWS, :].astype(jnp.float32)
    position_ref[...] = own[1:2].astype(jnp.int32)
    scale_ref[...] = (own[2:3] + own[3:4]) + own[4:5]


def join_kernel(parts_ref, out_ref):
    panel = (parts_ref[0] + parts_ref[1]).astype(jnp.bfloat16)
    for peer in range(out_ref.shape[0]):
        out_ref[peer] = panel


def attend_kernel(
    table_any, scale_ref, got_ref, panel_ref, out_ref,
    query_ref, score_ref, prob_ref, total_ref, values_ref, full_ref, table_ref, sem,
):
    fetch = pltpu.make_async_copy(table_any, table_ref, sem)
    fetch.start()
    scale = scale_ref[:, 0:1] * (math.log2(math.e) / math.sqrt(HEAD_DIM))
    low = low_lanes(HALF)
    for source in range(SOURCES):
        tile = got_ref[source, 2 * HALF:TAIL]
        zero = jnp.zeros_like(tile)
        query_ref[source * BLOCK:source * BLOCK + HALF] = jnp.where(low, tile, zero)
        query_ref[source * BLOCK + HALF:source * BLOCK + BLOCK] = jnp.where(low, swap_halves(tile), zero)

    def finish(source, weighted, denominator):
        attended = (weighted / denominator).astype(jnp.bfloat16)
        out_ref[source] = jnp.where(low, swap_halves(attended[0:HALF]), attended[HALF:BLOCK])

    def blocks_of(source):
        return jnp.concatenate([panel_ref[table_ref[source, j]] for j in range(LISTED)], axis=0)

    for block in range(GROUP):
        turned = jnp.transpose(panel_ref[block].astype(jnp.float32))
        values_ref[block] = turned[HALF:BLOCK].astype(jnp.bfloat16)
    fetch.wait()
    dense = table_ref[0, GROUP] > LISTED * BLOCK

    @pl.when(jnp.logical_not(dense))
    def _():
        for source in range(SOURCES):
            rows = slice(source * BLOCK, source * BLOCK + BLOCK)
            score = lax.dot_general(
                query_ref[rows], blocks_of(source), CONTRACT_LAST, preferred_element_type=jnp.float32
            )
            column = lax.broadcasted_iota(jnp.int32, score.shape, 1)
            score_ref[rows] = jnp.where(column < table_ref[source, GROUP], score, -jnp.inf)
        scores = score_ref[...]
        weights = jnp.exp2((scores - jnp.max(scores, axis=-1, keepdims=True)) * scale)
        total_ref[...] = jnp.broadcast_to(jnp.sum(weights, axis=-1, keepdims=True), total_ref.shape)
        prob_ref[...] = weights.astype(jnp.bfloat16)
        for source in range(SOURCES):
            rows = slice(source * BLOCK, source * BLOCK + BLOCK)
            weighted = jnp.dot(prob_ref[rows], blocks_of(source), preferred_element_type=jnp.float32)
            finish(source, weighted, total_ref[rows])

    @pl.when(dense)
    def _():
        span = PER_DOT * BLOCK
        chunks = range(0, GROUP, CHUNK)

        def score(first, chunk):
            query = query_ref[first * BLOCK:first * BLOCK + span]
            keys = panel_ref[chunk:chunk + CHUNK].reshape(CHUNK * BLOCK, 128)
            rows = slice(chunk * BLOCK, (chunk + CHUNK) * BLOCK)
            full_ref[rows, first * BLOCK:first * BLOCK + span] = lax.dot_general(
                keys, query, CONTRACT_LAST, preferred_element_type=jnp.float32
            )

        for chunk in chunks:
            score(0, chunk)
        for first in range(0, SOURCES, PER_DOT):
            columns = slice(first * BLOCK, first * BLOCK + span)
            top = jnp.max(full_ref[:, columns], axis=0, keepdims=True)
            total, weighted = 0.0, 0.0
            for chunk in chunks:
                rows = slice(chunk * BLOCK, (chunk + CHUNK) * BLOCK)
                if first + PER_DOT < SOURCES:
                    score(first + PER_DOT, chunk)
                weights = jnp.exp2((full_ref[rows, columns] - top) * scale)
                total = total + jnp.sum(weights, axis=0, keepdims=True)
                values = jnp.concatenate([values_ref[chunk + k] for k in range(CHUNK)], axis=1)
                weighted = weighted + jnp.dot(
                    values, weights.astype(jnp.bfloat16), preferred_element_type=jnp.float32
                )
            attended = weighted / total
            for k in range(PER_DOT):
                piece = attended[:, k * BLOCK:k * BLOCK + BLOCK]
                piece = jnp.transpose(jnp.concatenate([piece, swap_halves(piece)], axis=0))
                out_ref[first + k] = piece[0:HALF].astype(jnp.bfloat16)


def finish_kernel(got_ref, wo_ref, feat_ref, position_ref, out_ref):
    low = low_lanes(HALF)
    upper, lower = [], []
    for pair in range(HEADS // 2):
        even, odd = got_ref[2 * pair], got_ref[2 * pair + 1]
        upper.append(jnp.where(low, even, swap_halves(odd)))
        lower.append(jnp.where(low, swap_halves(even), odd))
    attended = jnp.concatenate([jnp.concatenate(upper, axis=1), jnp.concatenate(lower, axis=1)], axis=0)
    product = jnp.dot(attended, wo_ref[...], preferred_element_type=jnp.float32)
    updated = (feat_ref[...].astype(jnp.float32) + product).astype(jnp.bfloat16)
    slot = lax.broadcasted_iota(jnp.int32, (BLOCK, BLOCK), 0)
    chosen = (slot == position_ref[...]).astype(jnp.float32).astype(jnp.bfloat16)
    moved = jnp.dot(chosen, updated, preferred_element_type=jnp.float32)
    out_ref[...] = moved.reshape(out_ref.shape).astype(jnp.bfloat16)


def shards(grid_feat, latent, query_gain, w_q, w_kv, w_o, head_scale, block_lists, list_len, dest):
    local_rows, width = grid_feat.shape
    bf16, f32, i32 = jnp.bfloat16, jnp.float32, jnp.int32
    shaped = jax.ShapeDtypeStruct

    packed = pl.pallas_call(
        pack_kernel,
        out_shape=shaped((HEADS, ROWS, 128), bf16),
        in_specs=[HBM] * 9,
        out_specs=VMEM,
        scratch_shapes=[
            pltpu.VMEM((local_rows, width), bf16),
            pltpu.VMEM((1, width), f32),
            pltpu.VMEM(latent.shape[::-1], bf16),
            pltpu.VMEM(w_kv.shape, bf16),
            pltpu.VMEM(w_q.shape, bf16),
            pltpu.VMEM((1, GROUP), i32),
            pltpu.VMEM((1, 1), i32),
            pltpu.VMEM((1, local_rows), i32),
            pltpu.VMEM((1, HEADS), f32),
            pltpu.VMEM((1, 128), i32),
            pltpu.SemaphoreType.DMA((9,)),
        ],
        name="pack",
        compiler_params=pltpu.CompilerParams(vmem_limit_bytes=12 << 20),
    )(
        *(
            pltpu.with_memory_space_constraint(x, pltpu.HBM)
            for x in (grid_feat, query_gain.reshape(1, -1), latent.T, w_kv, w_q, block_lists)
        ),
        list_len.reshape(1, 1),
        pltpu.with_memory_space_constraint(dest.reshape(1, -1), pltpu.HBM),
        pltpu.with_memory_space_constraint(head_scale.reshape(1, -1), pltpu.HBM),
    )
    got = lax.all_to_all(packed, "y", 0, 0, tiled=True)

    partial, table, position, scale = pl.pallas_call(
        project_kernel,
        out_shape=(
            shaped((BLOCK, 128), f32), shaped((SOURCES, 128), i32), shaped((1, 128), i32), shaped((1, 128), f32)
        ),
        in_specs=[VMEM],
        out_specs=(VMEM,) * 4,
        name="project",
        compiler_params=PARAMS,
    )(got)
    parts = lax.all_gather(partial, "xl", axis=0)
    panel = pl.pallas_call(
        join_kernel,
        out_shape=shaped((GROUP // 2, BLOCK, 128), bf16),
        in_specs=[VMEM],
        out_specs=VMEM,
        name="join",
        compiler_params=PARAMS,
    )(parts)
    panels = lax.all_to_all(panel, "z", 0, 0, tiled=True)
    panels = lax.all_gather(panels, "c", axis=0).reshape(GROUP, BLOCK, 128)

    attended = pl.pallas_call(
        attend_kernel,
        out_shape=shaped((SOURCES, HALF, 128), bf16),
        in_specs=[ANY, VMEM, VMEM, VMEM],
        out_specs=VMEM,
        scratch_shapes=[
            pltpu.VMEM((SOURCES * BLOCK, 128), bf16),
            pltpu.VMEM((SOURCES * BLOCK, LISTED * BLOCK), f32),
            pltpu.VMEM((SOURCES * BLOCK, LISTED * BLOCK), bf16),
            pltpu.VMEM((SOURCES * BLOCK, 128), f32),
            pltpu.VMEM((GROUP, HALF, BLOCK), bf16),
            pltpu.VMEM((GROUP * BLOCK, SOURCES * BLOCK), f32),
            pltpu.SMEM((SOURCES, 128), i32),
            pltpu.SemaphoreType.DMA,
        ],
        name="attend",
        compiler_params=PARAMS,
    )(table, scale, got, panels)
    attended = lax.all_to_all(attended, "y", 0, 0, tiled=True)

    outgoing = pl.pallas_call(
        finish_kernel,
        out_shape=shaped((local_rows // 2, 2, width), bf16),
        in_specs=[VMEM] * 4,
        out_specs=VMEM,
        name="finish",
        compiler_params=PARAMS,
    )(attended, w_o, grid_feat, position)
    arrived = lax.all_to_all(outgoing, ("xh", "z", "c"), 0, 0, tiled=True)
    return arrived.reshape(local_rows, width)


def solution(mesh):
    fine = Mesh(mesh.devices.reshape(4, 8, 2, 2, 8), ("xh", "z", "c", "xl", "y"))
    band, sector = ("xh", "z", "c"), ("xl", "y")
    return jax.shard_map(
        shards,
        mesh=fine,
        in_specs=(
            P(band + sector, None),
            P(band, sector),
            P(),
            P(),
            P(sector, None),
            P(),
            P(),
            P(band + sector, None),
            P(band + sector),
            P(band + sector),
        ),
        out_specs=P(band + sector, None),
        check_vma=False,
    )
```
